32 devices in a mesh: groups: 2 (over y), match: 4 (over x, core), dp: 4 (over z).
Axes of the slice: x: 2, y: 2, z: 4, core: 2. Of those that a mesh axis runs over, the one named last changes fastest.
Arguments:
- query_states: bfloat16 [128, 128, 2048], P(('groups', 'match', 'dp')), parts along dimension 0, may hold values from -6 to 6
- formal_states: bfloat16 [128, 128, 2048], P(('groups', 'match', 'dp')), parts along dimension 0, may hold values from -6 to 6
- projection: bfloat16 [2048, 128], replicated, may hold values from -0.125 to 0.125
- query_len: int32 [128], P(('groups', 'match', 'dp')), parts along dimension 0, may hold values from 32 to 128
- formal_len: int32 [128], P(('groups', 'match', 'dp')), parts along dimension 0, may hold values from 32 to 128
- positives: int32 [32, 4], P(('groups', 'match', 'dp')), parts along dimension 0, may hold values from 0 to 3, each once within a row
- offsets: int32 [6], P('groups'), parts along dimension 0, may hold values from 1 to 3, as said below
Outputs:
- scores: float32 [128, 16], P(('groups', 'match', 'dp')), parts along dimension 0
- query_loss: float32 [128], P(('groups', 'match', 'dp')), parts along dimension 0
- weight_grad: float32 [4096, 128], P(('groups', 'dp')), parts along dimension 0
The draws below stay inside these ranges and needn't reach their ends.
There are 2 independent parts, one for each index of `groups`. The reference program is written for one: setup_inputs(seed, part) draws one part's arguments, and reference() takes and returns one part's arrays. A program takes and returns all parts, laid end to end along the dimension named above; an argument that names none is the same for every part. Nothing has to cross between parts.
Inputs may be any that keep to these rules, and one draw needn't show every extreme that they name: The 3 offsets are distinct.
All inputs are finite; a program needn't handle non-finite values.
Results may differ from the reference program's by a relative error of at most 0.015.
Values may be sent and summed in bfloat16 or wider, within the bound.
A program may use at most 64 MiB of HBM per device.

```python
import jax
import jax.numpy as jnp
from jax import lax

Q_DEV = 4
L = 128
H = 2048
E = 128
ROUNDS = 3
SHARDS = 16
STATEMENTS = 64
CANDS = 16
N_MATCH = 4
N_DP = 4


def draw_offsets(key, part):
    own_key = jax.random.fold_in(key, 7919)
    ranks = jax.random.randint(own_key, (N_MATCH - 1,), 0, 1 << 20, dtype=jnp.int32)
    keyed = ranks * 128 + jnp.arange(N_MATCH - 1, dtype=jnp.int32)
    order = jnp.argsort(keyed, stable=True).astype(jnp.int32)
    return (order[:ROUNDS] + 1).astype(jnp.int32)


def plant(drawn, rng, low, largest):
    longest = drawn.shape.index(max(drawn.shape))
    spots = []
    for shift in (0, 1):
        where = [jax.random.randint(jax.random.fold_in(rng, axis), (), 0, length) for axis, length in enumerate(drawn.shape)]
        where[longest] = (where[longest] + shift) % drawn.shape[longest]
        spots.append(tuple(where))
    return drawn.at[spots[0]].set(low).at[spots[1]].set(largest)


def with_spikes(result, rng, source, target, shards_of, factor):
    def block_of(axis_at):
        return (jnp.arange(result.shape[axis_at]) // (result.shape[axis_at] // shards_of)).reshape((-1,) + (1,) * (result.ndim - 1 - axis_at))

    one_side = jax.random.permutation(rng, shards_of)[block_of(target)]
    other_side = (block_of(target) + shards_of // 2) % shards_of
    return jnp.where((block_of(source) == one_side) | (block_of(source) == other_side), factor * result, result)


def block_scale(stream_key, extent, shards, smallest, top_value):
    gain, own = 1.0, jax.random.fold_in(stream_key, 6)
    for dim, parts in shards:
        heights = jnp.exp(jax.random.uniform(jax.random.fold_in(own, dim), (parts,), jnp.float32, smallest / len(shards), top_value / len(shards)))
        gain = gain * jnp.repeat(heights, extent[dim] // parts).reshape([-1 if axis == dim else 1 for axis in range(len(extent))])
    return gain


def bell_draw(stream_key, shape, scale, bound, cuts=(), held_as=jnp.bfloat16):
    array = scale * jax.random.normal(stream_key, shape, jnp.float32)
    if cuts:
        array = array * block_scale(stream_key, shape, cuts, -0.22, 0.18)
    return jnp.clip(array, -bound, bound).astype(held_as)


def bell_draw_with(key, shape, width, limit, pieces, heavy, held_as=jnp.bfloat16):
    entries = width * jax.random.normal(key, shape, jnp.float32)
    if pieces:
        entries = entries * block_scale(key, shape, pieces, -0.22, 0.18)
    return jnp.clip(with_spikes(entries, jax.random.fold_in(key, 3), *heavy), -limit, limit).astype(held_as)


def setup_inputs(seed: int = 0, part: int = 0) -> dict:
    key_of = jax.random.split(jax.random.key(seed), 8)
    own_keys = jax.random.split(jax.random.fold_in(key_of[7], part), 8)
    query_states = bell_draw_with(own_keys[0], (STATEMENTS, L, H), 1.0, 6.0, ((0, 16),), (0, 2, 16, 2.0))
    formal_states = bell_draw_with(own_keys[1], (STATEMENTS, L, H), 1.0, 6.0, ((0, 16),), (0, 2, 16, 2.0))
    projection = bell_draw(key_of[2], (H, E), H ** -0.5, 0.125)
    query_len = plant(jax.random.randint(own_keys[3], (STATEMENTS,), L // 4, L + 1), jax.random.fold_in(own_keys[3], 1), L // 4, L).astype(jnp.int32)
    formal_len = plant(jax.random.randint(own_keys[4], (STATEMENTS,), L // 4, L + 1), jax.random.fold_in(own_keys[4], 1), L // 4, L).astype(jnp.int32)
    positives = jax.vmap(lambda own: jax.random.permutation(own, Q_DEV))(jax.random.split(own_keys[5], SHARDS)).reshape((SHARDS, Q_DEV)).astype(jnp.int32)
    offsets = draw_offsets(jax.random.fold_in(jax.random.fold_in(key_of[7], part), 71), part)
    return dict(query_states=query_states, formal_states=formal_states, projection=projection, query_len=query_len, formal_len=formal_len, positives=positives, offsets=offsets)


token_temp = 0.05
match_temp = 0.05
norm_eps = 1e-06

def project_tokens(states, projection):
    flattened = states.reshape(-1, states.shape[-1])
    raw_proj = jnp.dot(flattened, projection, preferred_element_type=jnp.float32)
    vector_norms = jnp.sqrt(lax.optimization_barrier(jnp.sum(raw_proj * raw_proj, axis=-1, keepdims=True)) + norm_eps)
    return (raw_proj / vector_norms, vector_norms)

def token_mask(lengths, span_size):
    return (jnp.arange(span_size, dtype=jnp.int32)[None, :] < lengths[:, None]).astype(jnp.float32)

def score_pairs(query_emb, query_len, cand_emb, cand_len):
    span_size = query_emb.shape[1]
    similar = jnp.einsum('qie,cje->qcij', query_emb.astype(jnp.float32), cand_emb.astype(jnp.float32))
    query_mask = token_mask(query_len, span_size)
    cand_mask = token_mask(cand_len, span_size)
    exp_sims = jnp.exp(similar / token_temp) * query_mask[:, None, :, None] * cand_mask[None, :, None, :]
    row_sums = lax.optimization_barrier(jnp.sum(exp_sims, 3)) + (1.0 - query_mask)[:, None, :]
    col_sums = lax.optimization_barrier(jnp.sum(exp_sims, 2)) + (1.0 - cand_mask)[None, :, :]
    query_tokens = query_len.astype(jnp.float32)
    cand_tokens = cand_len.astype(jnp.float32)
    forward = token_temp * lax.optimization_barrier(jnp.sum(jnp.log(row_sums), 2)) / query_tokens[:, None]
    reverse = token_temp * lax.optimization_barrier(jnp.sum(jnp.log(col_sums), 2)) / cand_tokens[None, :]
    scores = 0.5 * (forward + reverse)
    return (scores, exp_sims, row_sums * query_tokens[:, None, None], col_sums * cand_tokens[None, :, None])

def contrast(scores, target):
    logits = scores / match_temp
    exp_logits = jnp.exp(logits)
    totals = lax.optimization_barrier(jnp.sum(exp_logits, 1))
    onehot = (jnp.arange(scores.shape[1], dtype=jnp.int32)[None, :] == target[:, None]).astype(jnp.float32)
    losses = jnp.log(totals) - lax.optimization_barrier(jnp.sum(onehot * logits, 1))
    score_grad = (exp_logits / totals[:, None] - onehot) / match_temp
    return (losses, score_grad)

def pair_grads(score_grad, exp_sims, row_scale, col_scale, query_emb, cand_emb):
    factor = 1.0 / row_scale[:, :, :, None] + 1.0 / col_scale[:, :, None, :]
    sim_grad = (0.5 * score_grad[:, :, None, None] * exp_sims * factor).astype(jnp.bfloat16)
    sim_wide = sim_grad.astype(jnp.float32)
    query_grad = jnp.einsum('qcij,cje->qie', sim_wide, cand_emb.astype(jnp.float32))
    cand_grad = jnp.einsum('qcij,qie->cje', sim_wide, query_emb.astype(jnp.float32))
    return (query_grad, cand_grad)

def unit_back(unit, vector_norms, grad):
    inner = lax.optimization_barrier(jnp.sum(unit * grad, axis=-1, keepdims=True))
    return ((grad - unit * inner) / vector_norms).astype(jnp.bfloat16)

def token_dot(left, right):
    return lax.dot_general(left, right, (((0,), (0,)), ((), ())), preferred_element_type=jnp.float32)

def reference(query_states, formal_states, projection, query_len, formal_len, positives, offsets):
    query_unit, query_norm = project_tokens(query_states, projection)
    formal_unit, formal_norm = project_tokens(formal_states, projection)
    query_emb = query_unit.astype(jnp.bfloat16).reshape(SHARDS, Q_DEV, L, E)
    formal_emb = formal_unit.astype(jnp.bfloat16).reshape(N_MATCH, N_DP, Q_DEV, L, E)
    formal_lens = formal_len.reshape(N_MATCH, N_DP, Q_DEV)
    cand_list = [formal_emb]
    len_list = [formal_lens]
    for number in range(ROUNDS):
        cand_list.append(jnp.roll(formal_emb, offsets[number], axis=0))
        len_list.append(jnp.roll(formal_lens, offsets[number], axis=0))
    cand_emb = jnp.stack(cand_list, 2).reshape(SHARDS, CANDS, L, E)
    cand_len = jnp.stack(len_list, 2).reshape(SHARDS, CANDS)

    def per_block(inputs):
        block_query, block_qlen, block_cand, block_clen, block_target = inputs
        scores, exp_sims, row_scale, col_scale = score_pairs(block_query, block_qlen, block_cand, block_clen)
        losses, score_grad = contrast(scores, block_target)
        query_grad, cand_grad = pair_grads(score_grad, exp_sims, row_scale, col_scale, block_query, block_cand)
        return (scores, losses, query_grad, cand_grad)
    scores, losses, query_grad, cand_grad = lax.map(per_block, (query_emb, query_len.reshape(SHARDS, Q_DEV), cand_emb, cand_len, positives))
    cand_grad = cand_grad.reshape(N_MATCH, N_DP, ROUNDS + 1, Q_DEV, L, E)
    formal_grad = cand_grad[:, :, 0]
    for number in range(ROUNDS):
        rounded = lax.optimization_barrier(cand_grad[:, :, number + 1].astype(jnp.bfloat16)).astype(jnp.float32)
        formal_grad = formal_grad + jnp.roll(rounded, -offsets[number], axis=0)
    query_raw = unit_back(query_unit, query_norm, query_grad.reshape(-1, E))
    formal_raw = unit_back(formal_unit, formal_norm, formal_grad.reshape(-1, E))
    weight_grad = token_dot(query_states.reshape(-1, H), query_raw) + token_dot(formal_states.reshape(-1, H), formal_raw)
    return (scores.reshape(STATEMENTS, CANDS), losses.reshape(STATEMENTS), weight_grad)
```

```python
import functools
import math

import jax
import jax.numpy as jnp
from jax import lax
from jax.experimental import pallas as pl
from jax.experimental.pallas import tpu as pltpu
from jax.sharding import PartitionSpec as P

MESH = pl.DeviceIdType.MESH
F32 = jnp.float32
BF16 = jnp.bfloat16
PIECES = 2
EXTRA = 16


def dot(left, right):
    return lax.dot_general(left, right, (((1,), (0,)), ((), ())), preferred_element_type=F32)


def dot_nt(left, right):
    return lax.dot_general(left, right, (((1,), (1,)), ((), ())), preferred_element_type=F32)


def fused(count, span, n_dp, rounds, *refs):
    (q_hbm, f_hbm, p_hbm, qlen_hbm, flen_hbm, pos_hbm, off_hbm, scores_ref, loss_ref, dw_ref,
     qv, fv, pv, cand, qemb, qembt, qunit, qinv, fraw, ex, rowm, colm, clens, gmat, qgrad,
     gsend, grecv, fgrad, acc, s1, r1, keep2, s2, r2, keep3, s3, r3, gat,
     qlen, flen, pos, off, in_sem, small_sem, cs_sem, cr_sem, gs_sem, gr_sem, s1_sem, r1_sem, s2_sem, r2_sem, s3_sem, r3_sem,
     s4_sem, r4_sem) = refs
    tokens = count * span
    embed = p_hbm.shape[1]
    hidden = p_hbm.shape[0]
    blocks = rounds + 1
    cands = blocks * count
    me = lax.axis_index("match")
    my_dp = lax.axis_index("dp")
    core = lax.rem(me, 2)
    side = me // 2
    partner = [
        me,
        side * 2 + (1 - core),
        (1 - side) * 2 + core,
        (1 - side) * 2 + (1 - core),
    ]

    def remote(src, dst, send, recv, where):
        return pltpu.make_async_remote_copy(
            src_ref=src, dst_ref=dst, send_sem=send, recv_sem=recv,
            device_id=where, device_id_type=MESH,
        )

    loads = [
        pltpu.make_async_copy(p_hbm, pv, in_sem.at[0]),
        pltpu.make_async_copy(q_hbm, qv, in_sem.at[1]),
    ]
    for n in range(PIECES):
        rows = pl.ds(n * (tokens // PIECES), tokens // PIECES)
        loads.append(pltpu.make_async_copy(f_hbm.at[rows, :], fv.at[rows, :], in_sem.at[2 + n]))
    smalls = [
        pltpu.make_async_copy(source, target, small_sem.at[n])
        for n, (source, target) in enumerate(
            ((flen_hbm, flen), (qlen_hbm, qlen), (pos_hbm, pos), (off_hbm, off))
        )
    ]
    for load in smalls + loads[:1] + loads[2:] + loads[1:2]:
        load.start()
    barrier = pltpu.get_barrier_semaphore()
    for x in range(1, 4):
        pl.semaphore_signal(barrier, inc=1, device_id={"match": partner[x]}, device_id_type=MESH)
    for d in range(1, n_dp):
        pl.semaphore_signal(
            barrier, inc=1, device_id={"dp": lax.rem(my_dp + d, n_dp)}, device_id_type=MESH
        )

    for load in smalls:
        load.wait()
    row_id = lax.broadcasted_iota(jnp.int32, (EXTRA, embed), 0)
    lens = jnp.zeros((EXTRA, embed), F32)
    for c in range(count):
        lens = jnp.where(row_id == c, flen[c].astype(F32), lens)
    cand[0, tokens:, :] = lens.astype(BF16)
    step = tokens // PIECES
    bounds = [
        pl.ds(n * step, step + EXTRA if n == PIECES - 1 else step) for n in range(PIECES)
    ]
    gathers = []
    loads[0].wait()
    for n in range(PIECES):
        rows = slice(n * step, (n + 1) * step)
        loads[2 + n].wait()
        raw = dot(fv[rows, :], pv[...])
        inv = lax.rsqrt(jnp.sum(raw * raw, axis=1, keepdims=True) + 1e-06)
        fraw[rows, :] = raw
        cand[0, rows, :] = (raw * inv).astype(BF16)
        if n == 0:
            pl.semaphore_wait(barrier, 3 + n_dp - 1)
        for x in (2, 1):
            copy = remote(
                cand.at[0, bounds[n], :], cand.at[x, bounds[n], :],
                cs_sem.at[x - 1, n], cr_sem.at[x - 1, n], {"match": partner[x]},
            )
            copy.start()
            gathers.append((x, copy))

    loads[1].wait()
    raw = dot(qv[...], pv[...])
    inv = lax.rsqrt(jnp.sum(raw * raw, axis=1, keepdims=True) + 1e-06)
    unit = raw * inv
    qunit[...] = unit
    qinv[...] = inv
    qemb[...] = unit.astype(BF16)
    qembt[...] = unit.T.astype(BF16)

    lane = lax.broadcasted_iota(jnp.int32, (span, span), 1)
    sub = lax.broadcasted_iota(jnp.int32, (span, span), 0)
    lane_row = lax.broadcasted_iota(jnp.int32, (1, span), 1)
    lane_f = lane_row.astype(F32)
    scale = math.log2(math.e) / 0.05

    def first_pass(b):
        lens = cand[b, tokens:, :].astype(F32)
        clens[b * count : (b + 1) * count, :] = lens[:count, :]

        def one(q, carry):
            rows = pl.ds(pl.multiple_of(q * span, span), span)
            query = qemb[rows, :]
            valid = sub < qlen[q]
            sums = jnp.zeros((span, span), F32) if b == 0 else rowm[rows, :]
            for c in range(count):
                similar = dot_nt(query, cand[b, c * span : (c + 1) * span, :])
                both = jnp.logical_and(valid, lane_f < lens[c : c + 1, :])
                val = jnp.where(both, jnp.exp2(similar * scale), 0.0)
                ex[b, rows, c * span : (c + 1) * span] = val
                sums = jnp.where(lane == b * count + c, jnp.sum(val, 1, keepdims=True), sums)
                colm[q, b * count + c : b * count + c + 1, :] = jnp.sum(val, 0, keepdims=True)
            rowm[rows, :] = sums
            return carry

        lax.fori_loop(0, count, one, 0, unroll=True)

    first_pass(0)
    for x, copy in gathers:
        if x == 1:
            copy.wait_recv()
    first_pass(1)
    forwards = []
    for n, copy in enumerate([copy for x, copy in gathers if x == 2]):
        copy.wait_recv()
        onward = remote(
            cand.at[2, bounds[n], :], cand.at[3, bounds[n], :],
            cs_sem.at[2, n], cr_sem.at[2, n], {"match": partner[1]},
        )
        onward.start()
        forwards.append(onward)
    first_pass(2)
    for onward in forwards:
        onward.wait_recv()
    first_pass(3)

    clen = clens[...]
    cand_ids = lax.broadcasted_iota(jnp.int32, (cands, span), 0)
    cand_lane = lax.broadcasted_iota(jnp.int32, (cands, span), 1)
    diag = cand_ids == cand_lane
    bad_col = jnp.where(cand_lane.astype(F32) < clen, 0.0, 1.0)
    for q in range(count):
        rows = slice(q * span, (q + 1) * span)
        query_tokens = jnp.full((1, span), qlen[q], jnp.int32).astype(F32)
        row_sums = rowm[rows, :] + jnp.where(sub < qlen[q], 0.0, 1.0)
        row_sums = jnp.where(lane < cands, row_sums, 1.0)
        col_sums = colm[q] + bad_col
        forward = jnp.sum(jnp.log(row_sums), 0, keepdims=True) / query_tokens
        reverse = jnp.sum(jnp.log(col_sums), 1, keepdims=True) / clen
        reverse = jnp.sum(jnp.where(diag, reverse, 0.0), 0, keepdims=True)
        logits = 0.5 * (forward + reverse)
        exps = jnp.where(lane_row < cands, jnp.exp(logits), 0.0)
        total = jnp.sum(exps, 1, keepdims=True)
        hot = jnp.where(lane_row == pos[0, q], 1.0, 0.0)
        loss = jnp.log(total) - jnp.sum(hot * logits, 1, keepdims=True)
        loss_ref[:, q : q + 1] = loss
        half_grad = (exps / total - hot) * (0.5 / 0.05)
        rowm[rows, :] = (half_grad / query_tokens) / row_sums
        turned = jnp.sum(jnp.where(diag, half_grad, 0.0), 1, keepdims=True)
        colm[q] = turned / (clen * col_sums)
        own = 0.05 * logits
        placed = jnp.where(lane_row < count, own, 0.0)
        for r in range(rounds):
            inside = jnp.logical_and(lane_row >= (r + 1) * count, lane_row < (r + 2) * count)
            for x in range(1, blocks):
                gap = lax.rem(me - partner[x] + blocks, blocks)
                moved = own if x == r + 1 else pltpu.roll(own, ((r + 1 - x) * count) % span, 1)
                here = jnp.logical_and(inside, jnp.full((1, span), off[r], jnp.int32) == gap)
                placed = jnp.where(here, moved, placed)
        scores_ref[q : q + 1, :] = placed[:, :cands]

    def second_pass(b, n, first=False):
        held = count // PIECES
        width = held * span
        cols = slice(n * width, (n + 1) * width)

        def one(q, carry):
            rows = pl.ds(pl.multiple_of(q * span, span), span)
            factors = rowm[rows, :]
            for c in range(n * held, (n + 1) * held):
                k = b * count + c
                mixed = factors[:, k : k + 1] + colm[q, k : k + 1, :]
                at = slice(c * span, (c + 1) * span)
                gmat[rows, at] = (ex[b, rows, at] * mixed).astype(BF16)
            return carry

        lax.fori_loop(0, count, one, 0, unroll=True)
        sim_grad = gmat[:, cols]
        cand_grad = dot(qembt[...], sim_grad)
        if b == 0:
            fgrad[:, cols] = cand_grad
        else:
            if b == 2:
                returns[3, n].wait_recv()
                cand_grad = cand_grad + grecv[2, n].astype(F32)
            gsend[b - 1, n] = cand_grad.astype(BF16)
            back = remote(
                gsend.at[b - 1, n], grecv.at[b - 1, n], gs_sem.at[b - 1, n], gr_sem.at[b - 1, n],
                {"match": partner[1 if b == 3 else b]},
            )
            back.start()
            returns[b, n] = back
        grad = dot(sim_grad, cand[b, cols, :])
        qgrad[...] = grad if first else qgrad[...] + grad

    returns = {}
    for b in (3, 2, 1, 0):
        for n in range(PIECES):
            second_pass(b, n, b == 3 and n == 0)

    unit = qunit[...]
    grad = qgrad[...]
    inner = jnp.sum(unit * grad, 1, keepdims=True)
    raw_grad = ((grad - unit * inner) * qinv[...]).T.astype(BF16)
    wide = hidden // n_dp // 2
    half = wide // 2
    for t in range(n_dp):
        for h in range(2):
            at = (t * 2 + h) * wide
            acc[t, h] = dot(raw_grad, qv[:, at : at + wide])

    raw = fraw[...].T
    inv = lax.rsqrt(jnp.sum(raw * raw, axis=0, keepdims=True) + 1e-06)
    unit = raw * inv
    grad = fgrad[...]
    for x in (1, 2):
        for n in range(PIECES):
            returns[x, n].wait_recv()
        grad = grad + jnp.concatenate([grecv[x - 1, n].astype(F32) for n in range(PIECES)], 1)
    inner = jnp.sum(unit * grad, 0, keepdims=True)
    raw_grad = ((grad - unit * inner) * inv).astype(BF16)

    def part(t, h):
        at = pl.multiple_of((t * 2 + h) * wide, wide)
        return acc[t, h] + dot(raw_grad, fv[:, pl.ds(at, wide)])

    order = [lax.rem(my_dp + d, n_dp) for d in list(range(1, n_dp)) + [0]]
    ones = []
    for n, t in enumerate(order):
        s1[n] = part(t, 1 - core).astype(BF16)
        copy = remote(s1.at[n], r1.at[n], s1_sem.at[n], r1_sem.at[n], {"match": partner[1]})
        copy.start()
        ones.append(copy)
    for n, t in enumerate(order):
        keep2[n] = part(t, core)
    twos = []
    for n in range(n_dp):
        ones[n].wait_recv()
        total = keep2[n] + r1[n].astype(F32)
        for s in range(2):
            piece = total[:, s * half : (s + 1) * half]
            keep3[n, s] = piece
            s2[n, s] = piece.astype(BF16)
        copy = remote(
            s2.at[n, 1 - side], r2.at[n], s2_sem.at[n], r2_sem.at[n], {"match": partner[2]}
        )
        copy.start()
        twos.append(copy)
    threes = []
    for n, t in enumerate(order):
        twos[n].wait_recv()
        total = keep3[n, side] + r2[n].astype(F32)
        if n < n_dp - 1:
            s3[n] = total.astype(BF16)
            copy = remote(s3.at[n], r3.at[n], s3_sem.at[n], r3_sem.at[n], {"dp": t})
            copy.start()
            threes.append(copy)
    for n in range(n_dp - 1):
        threes[n].wait_recv()
        total = total + r3[n].astype(F32)
    mine = core * 2 + side
    gat[mine] = total.T.astype(BF16)
    fours = []
    for x in (2, 3, 1):
        copy = remote(
            gat.at[mine], gat.at[mine], s4_sem.at[x - 1], r4_sem.at[x - 1], {"match": partner[x]}
        )
        copy.start()
        fours.append(copy)
    for copy in fours:
        copy.wait_recv()
    dw_ref[...] = gat[...].reshape(dw_ref.shape)
    for copy in [copy for _, copy in gathers] + forwards + list(returns.values()) + ones + twos + threes + fours:
        copy.wait_send()


def hand_over(scores_ref, loss_ref, dw_ref, scores_out, loss_out, dw_out):
    scores_out[...] = scores_ref[...]
    loss_out[...] = loss_ref[...]
    dw_out[...] = dw_ref[...].astype(F32)


def fused_body(n_dp, query_states, formal_states, projection, query_len, formal_len, positives, offsets):
    count, span, hidden = query_states.shape
    embed = projection.shape[1]
    rounds = offsets.shape[0]
    blocks = rounds + 1
    tokens = count * span
    cands = blocks * count
    wide = hidden // n_dp // 2
    half = wide // 2
    hbm = pl.BlockSpec(memory_space=pltpu.HBM)
    vmem = pl.BlockSpec(memory_space=pltpu.VMEM)
    dma = lambda n: pltpu.SemaphoreType.DMA((n,))
    scores, losses, rows = pl.pallas_call(
        functools.partial(fused, count, span, n_dp, rounds),
        name="contrastive_step",
        out_shape=(
            pltpu.VMEM((count, cands), F32),
            pltpu.VMEM((1, count), F32),
            pltpu.VMEM((hidden // n_dp, embed), BF16),
        ),
        in_specs=[hbm] * 7,
        out_specs=(vmem,) * 3,
        scratch_shapes=[
            pltpu.VMEM((tokens, hidden), BF16),
            pltpu.VMEM((tokens, hidden), BF16),
            pltpu.VMEM((hidden, embed), BF16),
            pltpu.VMEM((blocks, tokens + EXTRA, embed), BF16),
            pltpu.VMEM((tokens, embed), BF16),
            pltpu.VMEM((embed, tokens), BF16),
            pltpu.VMEM((tokens, embed), F32),
            pltpu.VMEM((tokens, 1), F32),
            pltpu.VMEM((tokens, embed), F32),
            pltpu.VMEM((blocks, tokens, tokens), F32),
            pltpu.VMEM((tokens, span), F32),
            pltpu.VMEM((count, cands, span), F32),
            pltpu.VMEM((cands, span), F32),
            pltpu.VMEM((tokens, tokens), BF16),
            pltpu.VMEM((tokens, embed), F32),
            pltpu.VMEM((rounds, PIECES, embed, tokens // PIECES), BF16),
            pltpu.VMEM((rounds, PIECES, embed, tokens // PIECES), BF16),
            pltpu.VMEM((embed, tokens), F32),
            pltpu.VMEM((n_dp, 2, embed, wide), F32),
            pltpu.VMEM((n_dp, embed, wide), BF16),
            pltpu.VMEM((n_dp, embed, wide), BF16),
            pltpu.VMEM((n_dp, embed, wide), F32),
            pltpu.VMEM((n_dp, 2, embed, half), BF16),
            pltpu.VMEM((n_dp, embed, half), BF16),
            pltpu.VMEM((n_dp, 2, embed, half), F32),
            pltpu.VMEM((n_dp - 1, embed, half), BF16),
            pltpu.VMEM((n_dp - 1, embed, half), BF16),
            pltpu.VMEM((4, half, embed), BF16),
            pltpu.SMEM(query_len.shape, jnp.int32),
            pltpu.SMEM(formal_len.shape, jnp.int32),
            pltpu.SMEM(positives.shape, jnp.int32),
            pltpu.SMEM(offsets.shape, jnp.int32),
            dma(2 + PIECES), dma(4), pltpu.SemaphoreType.DMA((3, PIECES)),
            pltpu.SemaphoreType.DMA((3, PIECES)), pltpu.SemaphoreType.DMA((3, PIECES)),
            pltpu.SemaphoreType.DMA((3, PIECES)),
            dma(n_dp), dma(n_dp), dma(n_dp), dma(n_dp), dma(n_dp - 1), dma(n_dp - 1),
            dma(3), dma(3),
        ],
        compiler_params=pltpu.CompilerParams(
            collective_id=0, has_side_effects=True, vmem_limit_bytes=56 << 20
        ),
    )(
        query_states.reshape(tokens, hidden), formal_states.reshape(tokens, hidden), projection,
        query_len, formal_len, positives, offsets,
    )
    scores, losses, rows = pl.pallas_call(
        hand_over,
        name="hand_over",
        out_shape=tuple(jax.ShapeDtypeStruct(x.shape, F32) for x in (scores, losses, rows)),
        in_specs=[vmem] * 3,
        out_specs=(vmem,) * 3,
    )(*(pltpu.with_memory_space_constraint(x, pltpu.VMEM) for x in (scores, losses, rows)))
    return scores, losses.reshape(-1), rows


token_temp = 0.05
match_temp = 0.05
norm_eps = 1e-06


def as_sent(shard):

    def short(part):
        return part.astype(jnp.bfloat16) if part.dtype == jnp.float32 else part

    return jax.tree.map(short, shard)


def shifted(value, axis, steps):
    count = lax.axis_size(axis)
    pairs = [(source, (source + steps) % count) for source in range(count)]
    return lax.ppermute(value, axis, pairs)


def project_tokens(states, projection):
    flattened = states.reshape(-1, states.shape[-1])
    raw_proj = jnp.dot(flattened, projection, preferred_element_type=jnp.float32)
    vector_norms = jnp.sqrt(jnp.sum(raw_proj * raw_proj, axis=-1, keepdims=True) + norm_eps)
    return (raw_proj / vector_norms, vector_norms)


def token_mask(lengths, span_size):
    return (jnp.arange(span_size, dtype=jnp.int32)[None, :] < lengths[:, None]).astype(jnp.float32)


def score_pairs(query_emb, query_len, cand_emb, cand_len):
    span_size = query_emb.shape[1]
    similar = jnp.einsum("qie,cje->qcij", query_emb, cand_emb, preferred_element_type=jnp.float32)
    query_mask = token_mask(query_len, span_size)
    cand_mask = token_mask(cand_len, span_size)
    exp_sims = (
        jnp.exp(similar / token_temp) * query_mask[:, None, :, None] * cand_mask[None, :, None, :]
    )
    row_sums = jnp.sum(exp_sims, 3) + (1.0 - query_mask)[:, None, :]
    col_sums = jnp.sum(exp_sims, 2) + (1.0 - cand_mask)[None, :, :]
    query_tokens = query_len.astype(jnp.float32)
    cand_tokens = cand_len.astype(jnp.float32)
    forward = token_temp * jnp.sum(jnp.log(row_sums), 2) / query_tokens[:, None]
    reverse = token_temp * jnp.sum(jnp.log(col_sums), 2) / cand_tokens[None, :]
    scores = 0.5 * (forward + reverse)
    return (
        scores,
        exp_sims,
        row_sums * query_tokens[:, None, None],
        col_sums * cand_tokens[None, :, None],
    )


def contrast(scores, target):
    logits = scores / match_temp
    exp_logits = jnp.exp(logits)
    totals = jnp.sum(exp_logits, 1)
    onehot = (jnp.arange(scores.shape[1], dtype=jnp.int32)[None, :] == target[:, None]).astype(
        jnp.float32
    )
    losses = jnp.log(totals) - jnp.sum(onehot * logits, 1)
    score_grad = (exp_logits / totals[:, None] - onehot) / match_temp
    return (losses, score_grad)


def pair_grads(score_grad, exp_sims, row_scale, col_scale, query_emb, cand_emb):
    factor = 1.0 / row_scale[:, :, :, None] + 1.0 / col_scale[:, :, None, :]
    sim_grad = (0.5 * score_grad[:, :, None, None] * exp_sims * factor).astype(jnp.bfloat16)
    query_grad = jnp.einsum("qcij,cje->qie", sim_grad, cand_emb, preferred_element_type=jnp.float32)
    cand_grad = jnp.einsum("qcij,qie->cje", sim_grad, query_emb, preferred_element_type=jnp.float32)
    return (query_grad, cand_grad)


def unit_back(unit, vector_norms, grad):
    inner = jnp.sum(unit * grad, axis=-1, keepdims=True)
    return ((grad - unit * inner) / vector_norms).astype(jnp.bfloat16)


def token_dot(left, right):
    return lax.dot_general(
        left, right, (((0,), (0,)), ((), ())), preferred_element_type=jnp.float32
    )


def rotate_docs(payload, stride):
    return shifted((payload[0], as_sent(payload[1])), "match", stride)


def return_grads(payload, stride):
    return shifted(payload, "match", stride)


def body(query_states, formal_states, projection, query_len, formal_len, positives, offsets):
    local_count, seq_tokens, hidden_width = query_states.shape
    embed_width = projection.shape[1]
    query_unit, query_norm = project_tokens(query_states, projection)
    formal_unit, formal_norm = project_tokens(formal_states, projection)
    query_emb = query_unit.astype(jnp.bfloat16).reshape(local_count, seq_tokens, embed_width)
    formal_emb = formal_unit.astype(jnp.bfloat16).reshape(local_count, seq_tokens, embed_width)
    rounds = offsets.shape[0]
    match_size = lax.axis_size("match")
    binary_digits = (match_size - 1).bit_length()
    chosen_docs = []
    chosen_lens = []
    for number in range(rounds):
        moving = (formal_emb, formal_len)
        for binary in range(binary_digits):
            arrived = rotate_docs(moving, 1 << binary)
            taken = offsets[number] // (1 << binary) % 2 == 1
            moving = (
                jnp.where(taken, arrived[0], moving[0]),
                jnp.where(taken, arrived[1], moving[1]),
            )
        chosen_docs.append(moving[0])
        chosen_lens.append(moving[1])
    cand_emb = jnp.concatenate([formal_emb] + chosen_docs, 0)
    cand_len = jnp.concatenate([formal_len] + chosen_lens, 0)
    target = positives.reshape(-1)
    scores, exp_sims, row_scale, col_scale = score_pairs(query_emb, query_len, cand_emb, cand_len)
    losses, score_grad = contrast(scores, target)
    query_grad, cand_grad = pair_grads(
        score_grad, exp_sims, row_scale, col_scale, query_emb, cand_emb
    )
    formal_grad = cand_grad[:local_count]
    for number in range(rounds):
        moving = cand_grad[(number + 1) * local_count : (number + 2) * local_count].astype(
            jnp.bfloat16
        )
        for binary in range(binary_digits):
            arrived = return_grads(moving, -(1 << binary))
            taken = offsets[number] // (1 << binary) % 2 == 1
            moving = jnp.where(taken, arrived, moving)
        formal_grad = formal_grad + moving.astype(jnp.float32)
    query_raw = unit_back(query_unit, query_norm, query_grad.reshape(-1, embed_width))
    formal_raw = unit_back(formal_unit, formal_norm, formal_grad.reshape(-1, embed_width))
    query_flat = query_states.reshape(-1, hidden_width)
    formal_flat = formal_states.reshape(-1, hidden_width)
    row_grad = lax.psum_scatter(
        (token_dot(query_flat, query_raw) + token_dot(formal_flat, formal_raw)).astype(
            jnp.bfloat16
        ),
        "dp",
        scatter_dimension=0,
        tiled=True,
    )
    weight_grad = lax.psum(row_grad, "match").astype(jnp.float32)
    return (scores, losses, weight_grad)


def solution(mesh):
    in_specs = (
        P(("groups", "match", "dp"), None, None),
        P(("groups", "match", "dp"), None, None),
        P(),
        P(("groups", "match", "dp")),
        P(("groups", "match", "dp")),
        P(("groups", "match", "dp"), None),
        P("groups"),
    )
    out_specs = (
        P(("groups", "match", "dp"), None),
        P(("groups", "match", "dp")),
        P(("groups", "dp"), None),
    )
    n_dp = mesh.shape["dp"]

    def chosen(*args):
        offsets, positives = args[6], args[5]
        blocks = offsets.shape[0] + 1
        if mesh.shape["match"] == blocks == 4 and n_dp > 1 and positives.shape == (1, args[0].shape[0]):
            return fused_body(n_dp, *args)
        return body(*args)

    return jax.shard_map(chosen, mesh=mesh, in_specs=in_specs, out_specs=out_specs, check_vma=False)
```
